32 devices in a mesh: group: 2 (over x), seq: 16 (over z, y, core).
Axes of the slice: x: 2, y: 2, z: 4, core: 2. Of those that a mesh axis runs over, the one named last changes fastest.
Arguments:
- hidden: bfloat16 [8, 256, 1408], P('group', 'seq'), parts along dimension 0, may hold values from -14 to 14
- skip: bfloat16 [8, 256, 1408], P('group', 'seq'), parts along dimension 0, may hold values from -6 to 6
- timestep: int32 [8], P('group'), parts along dimension 0, may hold values from 0 to 999
- w_skip: bfloat16 [2816, 1408], P('seq'), may hold values from -0.109375 to 0.109375
- w_mod: bfloat16 [256, 4224], replicated, may hold values from -5 to 5
- w_qkv: bfloat16 [1408, 4224], P('seq'), may hold values from -0.15625 to 0.15625
- w_out: bfloat16 [1408, 1408], P('seq'), may hold values from -0.15625 to 0.15625
Outputs:
- result: bfloat16 [8, 256, 1408], P('group', 'seq'), parts along dimension 0
The draws below stay inside these ranges and needn't reach their ends.
There are 2 independent parts, one for each index of `group`. The reference program is written for one: setup_inputs(seed, part) draws one part's arguments, and reference() takes and returns one part's arrays. A program takes and returns all parts, laid end to end along the dimension named above; an argument that names none is the same for every part. Nothing has to cross between parts.
All inputs are finite; a program needn't handle non-finite values.
Results may differ from the reference program's by a relative error of at most 0.0095.
Values may be sent and summed in bfloat16 or wider, within the bound.
A program may use at most 128 MiB of HBM per device.

```python
import math
import jax
import jax.numpy as jnp
from jax import lax

D = 1408
H = 16
HD = 88
TDIM = 256
SEQS = 4
LEN = 256


cluster_count = 8


def draw_hidden(key, part):
    key_center = jax.random.fold_in(key, 11)
    key_assign = jax.random.fold_in(key, 12)
    key_spread = jax.random.fold_in(key, 13)
    centers = jnp.clip(jax.random.normal(key_center, (SEQS, cluster_count, D), jnp.float32), -4.0, 4.0) * 2.0
    assign = jax.random.randint(key_assign, (SEQS, LEN), 0, cluster_count)
    picked = centers[jnp.arange(SEQS)[:, None], assign]
    spread_part = jnp.clip(jax.random.normal(key_spread, (SEQS, LEN, D), jnp.float32), -6.0, 6.0)
    return (picked + spread_part).astype(jnp.bfloat16)


def draw_w_mod(key, part):
    key_entries = jax.random.fold_in(key, 21)
    entries = jnp.clip(jax.random.normal(key_entries, (TDIM, 3 * D), jnp.float32), -4.0, 4.0)
    column_scale = jnp.where(jnp.arange(3 * D) >= 2 * D, 5.0, 1.0).astype(jnp.float32)
    return (entries * column_scale[None, :] * TDIM ** (-0.5)).astype(jnp.bfloat16)


def touch_ends(array, stream_key, smallest, largest):
    extent = array.shape
    index_at = [jax.random.randint(jax.random.fold_in(stream_key, axis), (), 0, extent[axis]) for axis in range(len(extent))]
    array = array.at[tuple(index_at)].set(smallest)
    longest = extent.index(max(extent))
    index_at[longest] = (index_at[longest] + 1) % extent[longest]
    return array.at[tuple(index_at)].set(largest)


def level_of(stream_key, extent, shards, smallest, largest):
    level = 1.0
    for dim, parts in shards:
        draws = jax.random.uniform(jax.random.fold_in(jax.random.fold_in(stream_key, 6), dim), (parts,), jnp.float32, smallest / len(shards), largest / len(shards))
        level = level * jnp.repeat(jnp.exp(draws), extent[dim] // parts).reshape((-1,) + (1,) * (len(extent) - 1 - dim))
    return level


def gaussian(rng, dims, scale, most, shards=(), kind=jnp.bfloat16):
    result = scale * jax.random.normal(rng, dims, jnp.float32)
    if shards:
        result = result * level_of(rng, dims, shards, -0.22, 0.18)
    return jnp.clip(result, -most, most).astype(kind)


def setup_inputs(seed: int = 0, part: int = 0) -> dict:
    seeds = jax.random.split(jax.random.key(seed), 8)
    own_keys = jax.random.split(jax.random.fold_in(seeds[7], part), 8)
    return {
        "hidden": draw_hidden(jax.random.fold_in(jax.random.fold_in(seeds[7], part), 71), part),
        "skip": gaussian(own_keys[1], (SEQS, LEN, D), 1.0, 6.0, ((1, 16),)),
        "timestep": touch_ends(jax.random.randint(own_keys[2], (SEQS,), 0, 1000), jax.random.fold_in(own_keys[2], 1), 0, 999).astype(jnp.int32),
        "w_skip": gaussian(seeds[3], (2 * D, D), (2 * D) ** -0.5, 0.109375, ((0, 16),)),
        "w_mod": draw_w_mod(jax.random.fold_in(seeds[7], 71), part),
        "w_qkv": gaussian(seeds[5], (D, 3 * D), D ** -0.5, 0.15625, ((0, 16),)),
        "w_out": gaussian(seeds[6], (D, D), D ** -0.5, 0.15625, ((0, 16),)),
    }


def layer_norm(x):
    mean = lax.optimization_barrier(jnp.mean(x, axis=-1, keepdims=True))
    var = lax.optimization_barrier(jnp.mean((x - mean) ** 2, axis=-1, keepdims=True))
    return (x - mean) * lax.rsqrt(var + 1e-06)

def reference(hidden, skip, timestep, w_skip, w_mod, w_qkv, w_out):
    combined = jnp.concatenate([hidden, skip], axis=2).reshape(SEQS * LEN, 2 * D)
    merged = jnp.dot(combined, w_skip, preferred_element_type=jnp.float32).astype(jnp.bfloat16)
    half = TDIM // 2
    freqs = jnp.exp(-math.log(10000.0) * jnp.arange(half, dtype=jnp.float32) / half)
    angles = timestep.astype(jnp.float32)[:, None] * freqs[None, :]
    embed = jnp.concatenate([jnp.cos(angles), jnp.sin(angles)], axis=1)
    act = jax.nn.silu(embed).astype(jnp.bfloat16)
    mod = jnp.dot(act, w_mod, preferred_element_type=jnp.float32)
    shift, scale, gate = (mod[:, :D], mod[:, D:2 * D], mod[:, 2 * D:])
    base = merged.astype(jnp.float32).reshape(SEQS, LEN, D)
    normed = (layer_norm(base) * (1.0 + scale[:, None, :]) + shift[:, None, :]).astype(jnp.bfloat16)
    qkv = jnp.dot(normed.reshape(SEQS * LEN, D), w_qkv, preferred_element_type=jnp.float32)
    qkv = qkv.reshape(SEQS, LEN, 3, H, HD)
    query = (layer_norm(qkv[:, :, 0]) * HD ** (-0.5)).astype(jnp.bfloat16)
    key = layer_norm(qkv[:, :, 1]).astype(jnp.bfloat16)
    value = qkv[:, :, 2].astype(jnp.bfloat16)
    query = jnp.transpose(query, (0, 2, 1, 3)).reshape(SEQS * H, LEN, HD)
    key = jnp.transpose(key, (0, 2, 1, 3)).reshape(SEQS * H, LEN, HD)
    value = jnp.transpose(value, (0, 2, 1, 3)).reshape(SEQS * H, LEN, HD)

    def attend(trio):
        qpair, kpair, vpair = trio
        scores = jnp.einsum('qd,kd->qk', qpair, kpair, preferred_element_type=jnp.float32)
        probs = jax.nn.softmax(scores, axis=-1).astype(jnp.bfloat16)
        return jnp.dot(probs, vpair, preferred_element_type=jnp.float32).astype(jnp.bfloat16)
    attended = lax.map(attend, (query, key, value))
    attended = jnp.transpose(attended.reshape(SEQS, H, LEN, HD), (0, 2, 1, 3)).reshape(SEQS * LEN, D)
    projected = jnp.dot(attended, w_out, preferred_element_type=jnp.float32).reshape(SEQS, LEN, D)
    return (base + gate[:, None, :] * projected).astype(jnp.bfloat16)
```

```python
import functools
import math

import jax
import jax.numpy as jnp
from jax import lax
from jax.sharding import PartitionSpec as P

H = 16
HD = 88
TDIM = 256


def layer_norm(x):
    mean = jnp.mean(x, axis=-1, keepdims=True)
    var = jnp.mean((x - mean) ** 2, axis=-1, keepdims=True)
    return (x - mean) * lax.rsqrt(var + 1e-06)


def attend_pair(trio):
    qpair, kpair, vpair = trio
    length = qpair.shape[0]
    block = min(512, length)
    qblocks = qpair.reshape(length // block, block, qpair.shape[1])

    def one_block(qblk):
        scores = jnp.einsum("qd,kd->qk", qblk, kpair, preferred_element_type=jnp.float32)
        probs = jax.nn.softmax(scores, axis=-1).astype(jnp.bfloat16)
        return jnp.dot(probs, vpair, preferred_element_type=jnp.float32).astype(jnp.bfloat16)

    return lax.map(one_block, qblocks).reshape(length, qpair.shape[1])


def to_heads(x, seqs, local):
    return jnp.transpose(x, (0, 2, 1, 3)).reshape(seqs * H, local, HD)


def gathered(hidden, skip, timestep, w_skip, w_mod, w_qkv, w_out):
    seqs, local, width = hidden.shape
    tok_rows = seqs * local
    combined = jnp.concatenate([hidden, skip], axis=2).reshape(tok_rows, 2 * width)
    full_skip = lax.all_gather(w_skip, "seq", axis=0, tiled=True)
    merged = jnp.dot(combined, full_skip, preferred_element_type=jnp.float32).astype(jnp.bfloat16)
    half = TDIM // 2
    freqs = jnp.exp(-math.log(10000.0) * jnp.arange(half, dtype=jnp.float32) / half)
    angles = timestep.astype(jnp.float32)[:, None] * freqs[None, :]
    embed = jnp.concatenate([jnp.cos(angles), jnp.sin(angles)], axis=1)
    act = jax.nn.silu(embed).astype(jnp.bfloat16)
    mod = jnp.dot(act, w_mod, preferred_element_type=jnp.float32)
    shift, scale, gate = (mod[:, :width], mod[:, width : 2 * width], mod[:, 2 * width :])
    base = merged.astype(jnp.float32).reshape(seqs, local, width)
    normed = (layer_norm(base) * (1.0 + scale[:, None, :]) + shift[:, None, :]).astype(jnp.bfloat16)
    normed = normed.reshape(tok_rows, width)
    full_qkv = lax.all_gather(w_qkv, "seq", axis=0, tiled=True)
    qkv = jnp.dot(normed, full_qkv, preferred_element_type=jnp.float32)
    qkv = qkv.reshape(seqs, local, 3, H, HD)
    query = (layer_norm(qkv[:, :, 0]) * HD ** (-0.5)).astype(jnp.bfloat16)
    key = layer_norm(qkv[:, :, 1]).astype(jnp.bfloat16)
    value = qkv[:, :, 2].astype(jnp.bfloat16)
    query = to_heads(query, seqs, local)
    key = to_heads(key, seqs, local)
    value = to_heads(value, seqs, local)
    query, key, value = (
        lax.all_to_all(query, "seq", split_axis=0, concat_axis=1, tiled=True),
        lax.all_to_all(key, "seq", split_axis=0, concat_axis=1, tiled=True),
        lax.all_to_all(value, "seq", split_axis=0, concat_axis=1, tiled=True),
    )
    attended = lax.map(attend_pair, (query, key, value))
    attended = lax.all_to_all(attended, "seq", split_axis=1, concat_axis=0, tiled=True)
    attended = jnp.transpose(attended.reshape(seqs, H, local, HD), (0, 2, 1, 3)).reshape(
        tok_rows, width
    )
    full_out = lax.all_gather(w_out, "seq", axis=0, tiled=True)
    projected = jnp.dot(attended, full_out, preferred_element_type=jnp.float32)
    projected = projected.reshape(seqs, local, width)
    return (base + gate[:, None, :] * projected).astype(jnp.bfloat16)


def modulation(timestep, w_mod):
    half = TDIM // 2
    freqs = jnp.exp(-math.log(10000.0) * jnp.arange(half, dtype=jnp.float32) / half)
    angles = timestep.astype(jnp.float32)[:, None] * freqs[None, :]
    embed = jnp.concatenate([jnp.cos(angles), jnp.sin(angles)], axis=1)
    act = jax.nn.silu(embed).astype(jnp.bfloat16)
    return jnp.dot(act, w_mod, preferred_element_type=jnp.float32)


def head_split(n, hidden, skip, timestep, w_skip, w_mod, w_qkv, w_out):
    seqs, local, width = hidden.shape
    rows = seqs * local
    heads = H // n
    combined = jnp.concatenate([hidden, skip], axis=2).reshape(rows, 2 * width)
    spread = lax.all_to_all(combined, "seq", split_axis=1, concat_axis=0, tiled=True)
    wq = w_qkv.reshape(w_qkv.shape[0], 3, n, heads * HD)
    wq = lax.all_to_all(wq, "seq", split_axis=2, concat_axis=0, tiled=True)
    wq = wq.reshape(width, 3 * heads * HD)
    part = jnp.dot(spread, w_skip, preferred_element_type=jnp.float32).astype(jnp.bfloat16)
    merged = lax.psum_scatter(part, "seq", scatter_dimension=0, tiled=True)
    mod = modulation(timestep, w_mod)
    shift, scale, gate = (mod[:, :width], mod[:, width : 2 * width], mod[:, 2 * width :])
    base = merged.astype(jnp.float32).reshape(seqs, local, width)
    normed = (layer_norm(base) * (1.0 + scale[:, None, :]) + shift[:, None, :]).astype(jnp.bfloat16)
    every = lax.all_gather(normed.reshape(rows, width), "seq", axis=0, tiled=True)
    qkv = jnp.dot(every, wq, preferred_element_type=jnp.float32)
    qkv = qkv.reshape(n, seqs, local, 3, heads, HD)
    query = (layer_norm(qkv[:, :, :, 0]) * HD ** (-0.5)).astype(jnp.bfloat16)
    key = layer_norm(qkv[:, :, :, 1]).astype(jnp.bfloat16)
    value = qkv[:, :, :, 2].astype(jnp.bfloat16)
    scores = jnp.einsum("mslhd,ntshd->shmlnt".replace("ntshd", "nsthd"), query, key, preferred_element_type=jnp.float32)
    shape = scores.shape
    probs = jax.nn.softmax(scores.reshape(shape[:4] + (-1,)), axis=-1).astype(jnp.bfloat16).reshape(shape)
    attended = jnp.einsum("shmlnt,nsthd->mslhd", probs, value, preferred_element_type=jnp.float32)
    attended = attended.astype(jnp.bfloat16).reshape(n * rows, heads * HD)
    part = jnp.dot(attended, w_out, preferred_element_type=jnp.float32).astype(jnp.bfloat16)
    projected = lax.psum_scatter(part, "seq", scatter_dimension=0, tiled=True)
    projected = projected.astype(jnp.float32).reshape(seqs, local, width)
    return (base + gate[:, None, :] * projected).astype(jnp.bfloat16)


def solution(mesh):
    n = mesh.shape["seq"]
    body = functools.partial(head_split, n) if H % n == 0 else gathered
    placed = (
        P("group", "seq", None),
        P("group", "seq", None),
        P("group"),
        P("seq", None),
        P(),
        P("seq", None),
        P("seq", None),
    )
    return jax.shard_map(
        body, mesh=mesh, in_specs=placed, out_specs=P("group", "seq", None), check_vma=False
    )
```
